32 devices in a mesh: dp: 8 (over z, x), mp: 4 (over y, core).
Axes of the slice: x: 2, y: 2, z: 4, core: 2. Of those that a mesh axis runs over, the one named last changes fastest.
Arguments:
- hidden_in: float32 [4096, 1024], P(('dp', 'mp')), may hold values from -6 to 6
- seg_ids: int32 [8, 512], P('dp'), may hold values from 0 to 7, never falling along the last dimension, each value on 1 to 128 neighbouring positions
- cotangent: float32 [4096, 1024], P(('dp', 'mp')), may hold values from -6 to 6
- w_qkv: float32 [2, 1024, 3072], P(None, 'dp', 'mp'), as said below
- w_dense: float32 [2, 1024, 1024], P(None, 'dp', 'mp'), may hold values from -0.5 to 0.5
- w_up: float32 [2, 1024, 4096], P(None, 'dp', 'mp'), may hold values from -0.1875 to 0.1875
- w_down: float32 [2, 1024, 4096], P(None, 'dp', 'mp'), may hold values from -0.09375 to 0.09375
- norm_gain: float32 [2, 2, 1024], replicated, may hold values from 0.5 to 1.5
- norm_bias: float32 [2, 2, 1024], replicated, may hold values from -2 to 2
- qkv_bias: float32 [2, 3072], replicated, may hold values from -2 to 2
- out_bias: float32 [2, 2, 1024], replicated, may hold values from -2 to 2
- up_bias: float32 [2, 4096], replicated, may hold values from -2 to 2
- qkv_moments: float32 [2, 2, 1024, 3072], P(None, None, 'dp', 'mp'), as said below
- dense_moments: float32 [2, 2, 1024, 1024], P(None, None, 'dp', 'mp'), as said below
- up_moments: float32 [2, 2, 1024, 4096], P(None, None, 'dp', 'mp'), as said below
- down_moments: float32 [2, 2, 1024, 4096], P(None, None, 'dp', 'mp'), as said below
- gain_moments: float32 [2, 2, 2, 1024], replicated, as said below
- nbias_moments: float32 [2, 2, 2, 1024], replicated, as said below
- qbias_moments: float32 [2, 2, 3072], replicated, as said below
- obias_moments: float32 [2, 2, 2, 1024], replicated, as said below
- ubias_moments: float32 [2, 2, 4096], replicated, as said below
Outputs:
- hidden_out: float32 [4096, 1024], P(('dp', 'mp'))
- hidden_grad: float32 [4096, 1024], P(('dp', 'mp'))
- qkv_grad: float32 [2, 1024, 3072], P(None, 'dp', 'mp')
- dense_grad: float32 [2, 1024, 1024], P(None, 'dp', 'mp')
- up_grad: float32 [2, 1024, 4096], P(None, 'dp', 'mp')
- down_grad: float32 [2, 1024, 4096], P(None, 'dp', 'mp')
- gain_grad: float32 [2, 2, 1024], replicated
- nbias_grad: float32 [2, 2, 1024], replicated
- qbias_grad: float32 [2, 3072], replicated
- obias_grad: float32 [2, 2, 1024], replicated
- ubias_grad: float32 [2, 4096], replicated
- qkv_new: float32 [2, 1024, 3072], P(None, 'dp', 'mp')
- dense_new: float32 [2, 1024, 1024], P(None, 'dp', 'mp')
- up_new: float32 [2, 1024, 4096], P(None, 'dp', 'mp')
- down_new: float32 [2, 1024, 4096], P(None, 'dp', 'mp')
- gain_new: float32 [2, 2, 1024], replicated
- nbias_new: float32 [2, 2, 1024], replicated
- qbias_new: float32 [2, 3072], replicated
- obias_new: float32 [2, 2, 1024], replicated
- ubias_new: float32 [2, 4096], replicated
- qkv_states: float32 [2, 2, 1024, 3072], P(None, None, 'dp', 'mp')
- dense_states: float32 [2, 2, 1024, 1024], P(None, None, 'dp', 'mp')
- up_states: float32 [2, 2, 1024, 4096], P(None, None, 'dp', 'mp')
- down_states: float32 [2, 2, 1024, 4096], P(None, None, 'dp', 'mp')
- gain_states: float32 [2, 2, 2, 1024], replicated
- nbias_states: float32 [2, 2, 2, 1024], replicated
- qbias_states: float32 [2, 2, 3072], replicated
- obias_states: float32 [2, 2, 2, 1024], replicated
- ubias_states: float32 [2, 2, 4096], replicated
The draws below stay inside these ranges and needn't reach their ends.
Inputs may be any that keep to these rules, and one draw needn't show every extreme that they name: `w_qkv`: columns of each head hold its query, then its key, then its value. `qkv_moments`: the first slice holds first moments, the second slice positive second moments. `dense_moments`: the first slice holds first moments, the second slice positive second moments. `up_moments`: the first slice holds first moments, the second slice positive second moments. `down_moments`: the first slice holds first moments, the second slice positive second moments. `gain_moments`: the first slice holds first moments, the second slice positive second moments. `nbias_moments`: the first slice holds first moments, the second slice positive second moments. `qbias_moments`: the first slice holds first moments, the second slice positive second moments. `obias_moments`: the first slice holds first moments, the second slice positive second moments. `ubias_moments`: the first slice holds first moments, the second slice positive second moments.
All inputs are finite; a program needn't handle non-finite values.
Results may differ from the reference program's by a relative error of at most 0.024.
Values may be sent and summed in bfloat16 or wider, within the bound.
A program may use at most 128 MiB of HBM per device.

```python
import math
import jax
import jax.numpy as jnp
import numpy as np
from jax import lax

D = 1024
HEADS = 16
FF = 4096
HD = 64
LEN = 512
LAYERS = 2
SEQS = 8
TOKENS = 4096


def draw_w_qkv(key, part):
    head_size = D // HEADS
    base = jax.random.normal(key, (LAYERS, D, HEADS, 3, head_size), jnp.float32)
    return (base * D ** (-0.5)).reshape(LAYERS, D, 3 * D)


def moment_pair(key, shape, tag):
    own_key = jax.random.fold_in(key, tag)
    first = jax.random.normal(jax.random.fold_in(own_key, 11), shape, jnp.float32)
    second = jnp.exp(jax.random.uniform(jax.random.fold_in(own_key, 12), shape, jnp.float32, math.log(0.03), 0.0))
    return jnp.stack([first, second])


def scaled_pair(key, shape, tag, scale):
    own_key = jax.random.fold_in(key, tag)
    first = jax.random.normal(jax.random.fold_in(own_key, 11), shape, jnp.float32) * (0.2 * scale)
    second = jnp.exp(jax.random.uniform(jax.random.fold_in(own_key, 12), shape, jnp.float32, math.log(0.0002), math.log(0.006))) * (scale * scale)
    return jnp.stack([first, second])


def draw_qkv_moments(key, part):
    return moment_pair(key, (LAYERS, D, 3 * D), 21)


def draw_dense_moments(key, part):
    return moment_pair(key, (LAYERS, D, D), 22)


def draw_up_moments(key, part):
    return moment_pair(key, (LAYERS, D, FF), 23)


def draw_down_moments(key, part):
    return moment_pair(key, (LAYERS, D, FF), 24)


def draw_gain_moments(key, part):
    return moment_pair(key, (LAYERS, 2, D), 25)


def draw_nbias_moments(key, part):
    root = math.sqrt(TOKENS)
    scale = (jnp.array([5.0, 0.6], jnp.float32) * root)[None, :, None]
    return scaled_pair(key, (LAYERS, 2, D), 26, scale)


def draw_qbias_moments(key, part):
    root = math.sqrt(TOKENS)
    return scaled_pair(key, (LAYERS, 3 * D), 27, 4.0 * root)


def draw_obias_moments(key, part):
    return moment_pair(key, (LAYERS, 2, D), 28)


def draw_ubias_moments(key, part):
    return moment_pair(key, (LAYERS, FF), 29)


def block_scale(stream_key, shape, split, low, top_value):
    gain, own = 1.0, jax.random.fold_in(stream_key, 6)
    for dim, parts in split:
        draws = jnp.exp(jax.random.uniform(jax.random.fold_in(own, dim), (parts,), jnp.float32, low / len(split), top_value / len(split)))
        gain = gain * jnp.repeat(draws, shape[dim] // parts).reshape([-1 if axis == dim else 1 for axis in range(len(shape))])
    return gain


def length_profile(amount, total, most, slope):
    loads = [(1 << 20) // math.isqrt(grade ** slope) + 1 for grade in range(2, amount + 1)]
    surplus, holding = total - most - (amount - 1), [1] * (amount - 1)
    while surplus > 0:
        candidates = [i for i in range(amount - 1) if holding[i] < most]
        pool, left = sum([loads[i] for i in candidates]), surplus
        for i in candidates:
            extra = min(most - holding[i], max(1, left * loads[i] // pool), surplus)
            holding[i] = holding[i] + extra
            surplus = surplus - extra
    return np.array([most] + holding)


def uneven_parts(rng, count, total, limit, lean):
    if count == 2:
        one = jax.random.randint(rng, (), max(1, total - limit), min(limit, total - 1) + 1)
        return jnp.stack([one, total - one])
    lengths = jnp.asarray(length_profile(count, total, limit, lean), jnp.int32)
    pairs = (count - 1) // 2
    giver, taker = lengths[1:1 + 2 * pairs:2], lengths[2:2 + 2 * pairs:2]
    slack = jnp.minimum(giver - 1, limit - taker)
    shifted = jax.random.randint(jax.random.fold_in(rng, 1), (pairs,), 0, 1 << 20) % (slack + 1)
    lengths = lengths.at[1:1 + 2 * pairs:2].set(giver - shifted).at[2:2 + 2 * pairs:2].set(taker + shifted)
    return lengths[jax.random.permutation(jax.random.fold_in(rng, 2), count)]


def scatter_about(rng, dims, width, bound, split=(), kind=jnp.bfloat16):
    drawn = width * jax.random.normal(rng, dims, jnp.float32)
    if split:
        drawn = drawn * block_scale(rng, dims, split, -0.22, 0.18)
    return jnp.clip(drawn, -bound, bound).astype(kind)


def setup_inputs(seed: int = 0) -> dict:
    key_list = jax.random.split(jax.random.key(seed), 22)
    hidden_in = scatter_about(key_list[0], (TOKENS, D), 1.0, 6.0, ((0, 32),), jnp.float32)
    seg_ids = jax.vmap(lambda own: jnp.searchsorted(jnp.cumsum(uneven_parts(own, 8, LEN, LEN // 4, 1)), jnp.arange(LEN), side="right"))(jax.random.split(key_list[1], SEQS)).reshape((SEQS, LEN)).astype(jnp.int32)
    cotangent = scatter_about(key_list[2], (TOKENS, D), 1.0, 6.0, ((0, 32),), jnp.float32)
    w_qkv = draw_w_qkv(jax.random.fold_in(key_list[21], 71), 0)
    w_dense = scatter_about(key_list[4], (LAYERS, D, D), (D // 8) ** -0.5, 0.5, ((1, 8), (2, 4)), jnp.float32)
    w_up = scatter_about(key_list[5], (LAYERS, D, FF), D ** -0.5, 0.1875, ((1, 8), (2, 4)), jnp.float32)
    w_down = scatter_about(key_list[6], (LAYERS, D, FF), FF ** -0.5, 0.09375, ((1, 8), (2, 4)), jnp.float32)
    norm_gain = jnp.clip(1.0 + 0.1 * jax.random.normal(key_list[7], (LAYERS, 2, D), jnp.float32), 0.5, 1.5)
    norm_bias = scatter_about(key_list[8], (LAYERS, 2, D), 0.3, 2.0, (), jnp.float32)
    qkv_bias = scatter_about(key_list[9], (LAYERS, 3 * D), 0.3, 2.0, (), jnp.float32)
    out_bias = scatter_about(key_list[10], (LAYERS, 2, D), 0.3, 2.0, (), jnp.float32)
    up_bias = scatter_about(key_list[11], (LAYERS, FF), 0.3, 2.0, (), jnp.float32)
    qkv_moments = draw_qkv_moments(jax.random.fold_in(key_list[21], 71), 0)
    dense_moments = draw_dense_moments(jax.random.fold_in(key_list[21], 71), 0)
    up_moments = draw_up_moments(jax.random.fold_in(key_list[21], 71), 0)
    down_moments = draw_down_moments(jax.random.fold_in(key_list[21], 71), 0)
    gain_moments = draw_gain_moments(jax.random.fold_in(key_list[21], 71), 0)
    nbias_moments = draw_nbias_moments(jax.random.fold_in(key_list[21], 71), 0)
    qbias_moments = draw_qbias_moments(jax.random.fold_in(key_list[21], 71), 0)
    obias_moments = draw_obias_moments(jax.random.fold_in(key_list[21], 71), 0)
    ubias_moments = draw_ubias_moments(jax.random.fold_in(key_list[21], 71), 0)
    return {"hidden_in": hidden_in, "seg_ids": seg_ids, "cotangent": cotangent, "w_qkv": w_qkv, "w_dense": w_dense, "w_up": w_up, "w_down": w_down, "norm_gain": norm_gain, "norm_bias": norm_bias, "qkv_bias": qkv_bias, "out_bias": out_bias, "up_bias": up_bias, "qkv_moments": qkv_moments, "dense_moments": dense_moments, "up_moments": up_moments, "down_moments": down_moments, "gain_moments": gain_moments, "nbias_moments": nbias_moments, "qbias_moments": qbias_moments, "obias_moments": obias_moments, "ubias_moments": ubias_moments}


norm_eps = 1e-05
beta_first = 0.9
beta_second = 0.999
adam_eps = 1e-08
learn_rate = 0.01
weight_decay = 0.1
adam_step = 3.0
gelu_scale = 0.7978845608028654
gelu_cubic = 0.044715

def layer_norm(values, gain_vec, shift_vec):
    centered = values - lax.optimization_barrier(jnp.mean(values, axis=-1, keepdims=True))
    inv_std = lax.rsqrt(lax.optimization_barrier(jnp.mean(centered * centered, axis=-1, keepdims=True)) + norm_eps)
    normed = centered * inv_std
    return (normed * gain_vec + shift_vec, normed, inv_std)

def norm_backward(upstream, normed, inv_std, gain_vec):
    scaled = upstream * gain_vec
    mean_one = lax.optimization_barrier(jnp.mean(scaled, axis=-1, keepdims=True))
    mean_two = lax.optimization_barrier(jnp.mean(scaled * normed, axis=-1, keepdims=True))
    return inv_std * (scaled - mean_one - normed * mean_two)

def gelu_parts(pre_act):
    inner_arg = gelu_scale * (pre_act + gelu_cubic * pre_act * pre_act * pre_act)
    tangent = jnp.tanh(inner_arg)
    result = 0.5 * pre_act * (1.0 + tangent)
    deriv = 0.5 * (1.0 + tangent) + 0.5 * pre_act * (1.0 - tangent * tangent) * gelu_scale * (1.0 + 3.0 * gelu_cubic * pre_act * pre_act)
    return (result, deriv)

def split_heads(joined):
    row_count = joined.shape[0]
    head_count = joined.shape[1] // (3 * HD)
    pieces = joined.reshape(row_count, head_count, 3, HD).astype(jnp.float32)
    return (pieces[:, :, 0], pieces[:, :, 1], pieces[:, :, 2])

def masked_scores(queries, key_rows, seg_row, slopes):
    row_count = queries.shape[0]
    scores = jnp.einsum('qhe,khe->hqk', queries, key_rows) * HD ** (-0.5)
    position = jnp.arange(row_count, dtype=jnp.int32)
    offset = (position[None, :] - position[:, None]).astype(jnp.float32)
    scores = scores + slopes[:, None, None] * offset[None]
    allowed = (position[None, :] <= position[:, None]) & (seg_row[:, None] == seg_row[None, :])
    return jnp.where(allowed[None], scores, -jnp.inf)

def attend(joined, seg_row, slopes):
    queries, key_rows, value_rows = split_heads(joined)
    scores = masked_scores(queries, key_rows, seg_row, slopes)
    highest = lax.optimization_barrier(jnp.max(scores, axis=-1, keepdims=True))
    log_total = highest + jnp.log(lax.optimization_barrier(jnp.sum(jnp.exp(scores - highest), axis=-1, keepdims=True)))
    weights = jnp.exp(scores - log_total).astype(jnp.bfloat16)
    mixed = jnp.einsum('hqk,khe->qhe', weights.astype(jnp.float32), value_rows)
    return (mixed.astype(jnp.bfloat16).reshape(joined.shape[0], -1), log_total)

def attend_backward(grad_mix, joined, mixed, log_total, seg_row, slopes):
    queries, key_rows, value_rows = split_heads(joined)
    row_count = joined.shape[0]
    head_count = queries.shape[1]
    scores = masked_scores(queries, key_rows, seg_row, slopes)
    probs = jnp.exp(scores - log_total)
    weights = probs.astype(jnp.bfloat16).astype(jnp.float32)
    grad_heads = grad_mix.reshape(row_count, head_count, HD).astype(jnp.float32)
    grad_values = jnp.einsum('hqk,qhe->khe', weights, grad_heads)
    grad_probs = jnp.einsum('qhe,khe->hqk', grad_heads, value_rows)
    delta = lax.optimization_barrier(jnp.sum(grad_heads * mixed.reshape(row_count, head_count, HD).astype(jnp.float32), axis=-1))
    grad_scores = (probs * (grad_probs - jnp.transpose(delta)[:, :, None])).astype(jnp.bfloat16).astype(jnp.float32)
    grad_queries = jnp.einsum('hqk,khe->qhe', grad_scores, key_rows) * HD ** (-0.5)
    grad_keys = jnp.einsum('hqk,qhe->khe', grad_scores, queries) * HD ** (-0.5)
    return jnp.stack([grad_queries, grad_keys, grad_values], axis=2).reshape(row_count, -1)

def forward_layer(stream_in, seg_row, matrices, vectors, slopes):
    w_joined, w_proj, w_expand, w_shrink = matrices
    gain_vec, shift_vec, joined_bias, out_shift, expand_bias = vectors
    normed_out, normed_one, inv_one = layer_norm(stream_in, gain_vec[0], shift_vec[0])
    rows_one = normed_out.astype(jnp.bfloat16)
    joined = (jnp.dot(rows_one, w_joined, preferred_element_type=jnp.float32) + joined_bias).astype(jnp.bfloat16)
    mixed, log_total = attend(joined, seg_row, slopes)
    middle = stream_in + jnp.dot(mixed, w_proj.T, preferred_element_type=jnp.float32) + out_shift[0]
    normed_mid, normed_two, inv_two = layer_norm(middle, gain_vec[1], shift_vec[1])
    rows_two = normed_mid.astype(jnp.bfloat16)
    pre_act = jnp.dot(rows_two, w_expand, preferred_element_type=jnp.float32) + expand_bias
    activated, deriv = gelu_parts(pre_act)
    hidden_act = activated.astype(jnp.bfloat16)
    result = middle + jnp.dot(hidden_act, w_shrink.T, preferred_element_type=jnp.float32) + out_shift[1]
    return (result, (normed_one, inv_one, rows_one, joined, mixed, log_total, normed_two, inv_two, rows_two, deriv, hidden_act))

def backward_layer(upstream, seg_row, matrices, vectors, saved, slopes):
    w_joined, w_proj, w_expand, w_shrink = matrices
    gain_vec, shift_vec, joined_bias, out_shift, expand_bias = vectors
    normed_one, inv_one, rows_one, joined, mixed, log_total, normed_two, inv_two, rows_two, deriv, hidden_act = saved
    grad_rows = upstream.astype(jnp.bfloat16)
    grad_hidden = jnp.dot(grad_rows, w_shrink, preferred_element_type=jnp.float32)
    shrink_part = jnp.dot(grad_rows.T, hidden_act, preferred_element_type=jnp.float32)
    grad_pre = grad_hidden * deriv
    pre_rounded = grad_pre.astype(jnp.bfloat16)
    expand_part = jnp.dot(rows_two.T, pre_rounded, preferred_element_type=jnp.float32)
    grad_norm_two = jnp.dot(pre_rounded, w_expand.T, preferred_element_type=jnp.float32)
    gain_two = lax.optimization_barrier(jnp.sum(grad_norm_two * normed_two, axis=0))
    shift_two = lax.optimization_barrier(jnp.sum(grad_norm_two, axis=0))
    middle = upstream + norm_backward(grad_norm_two, normed_two, inv_two, gain_vec[1])
    grad_rows_one = middle.astype(jnp.bfloat16)
    grad_mixed = jnp.dot(grad_rows_one, w_proj, preferred_element_type=jnp.float32).astype(jnp.bfloat16)
    proj_part = jnp.dot(grad_rows_one.T, mixed, preferred_element_type=jnp.float32)
    grad_joined = attend_backward(grad_mixed, joined, mixed, log_total, seg_row, slopes)
    joined_rounded = grad_joined.astype(jnp.bfloat16)
    joined_part = jnp.dot(rows_one.T, joined_rounded, preferred_element_type=jnp.float32)
    grad_norm_one = jnp.dot(joined_rounded, w_joined.T, preferred_element_type=jnp.float32)
    gain_one = lax.optimization_barrier(jnp.sum(grad_norm_one * normed_one, axis=0))
    shift_one = lax.optimization_barrier(jnp.sum(grad_norm_one, axis=0))
    grad_below = middle + norm_backward(grad_norm_one, normed_one, inv_one, gain_vec[0])
    grads = (joined_part, proj_part, expand_part, shrink_part, jnp.stack([gain_one, gain_two]), jnp.stack([shift_one, shift_two]), lax.optimization_barrier(jnp.sum(grad_joined, axis=0)), jnp.stack([lax.optimization_barrier(jnp.sum(middle, axis=0)), lax.optimization_barrier(jnp.sum(upstream, axis=0))]), lax.optimization_barrier(jnp.sum(grad_pre, axis=0)))
    return (grad_below, grads)

def adamw(weight, gradient, moments, decay):
    first = beta_first * moments[0] + (1.0 - beta_first) * gradient
    second = beta_second * moments[1] + (1.0 - beta_second) * gradient * gradient
    first_hat = first / (1.0 - beta_first ** adam_step)
    second_hat = second / (1.0 - beta_second ** adam_step)
    updated = weight - learn_rate * (first_hat / (jnp.sqrt(second_hat) + adam_eps) + decay * weight)
    return (updated, jnp.stack([first, second]))

def reference(hidden_in, seg_ids, cotangent, w_qkv, w_dense, w_up, w_down, norm_gain, norm_bias, qkv_bias, out_bias, up_bias, qkv_moments, dense_moments, up_moments, down_moments, gain_moments, nbias_moments, qbias_moments, obias_moments, ubias_moments):
    slopes = 2.0 ** (-8.0 * jnp.arange(1, HEADS + 1, dtype=jnp.float32) / HEADS)
    rounded = (w_qkv.astype(jnp.bfloat16), w_dense.astype(jnp.bfloat16), w_up.astype(jnp.bfloat16), w_down.astype(jnp.bfloat16))
    params = (norm_gain, norm_bias, qkv_bias, out_bias, up_bias)
    stream = hidden_in.reshape(SEQS, LEN, D)
    layer_inputs = []
    for layer_idx in range(LAYERS):
        layer_inputs.append(stream)
        matrices = tuple((stacked[layer_idx] for stacked in rounded))
        vectors = tuple((stacked[layer_idx] for stacked in params))

        def run_forward(scan_item, matrices=matrices, vectors=vectors):
            return forward_layer(scan_item[0], scan_item[1], matrices, vectors, slopes)[0]
        stream = lax.map(run_forward, (stream, seg_ids))
    upstream = cotangent.reshape(SEQS, LEN, D)
    layer_grads = [None] * LAYERS
    for layer_idx in reversed(range(LAYERS)):
        matrices = tuple((stacked[layer_idx] for stacked in rounded))
        vectors = tuple((stacked[layer_idx] for stacked in params))

        def run_back(totals, scan_item, matrices=matrices, vectors=vectors):
            stream_in, seg_row, grad_in = scan_item
            unused_out, saved = forward_layer(stream_in, seg_row, matrices, vectors, slopes)
            grad_below, grads = backward_layer(grad_in, seg_row, matrices, vectors, saved, slopes)
            return (tuple((left_term + right_term for left_term, right_term in zip(totals, grads))), grad_below)
        zero_init = tuple((jnp.zeros(entry.shape[1:], jnp.float32) for entry in (w_qkv, w_dense, w_up, w_down, norm_gain, norm_bias, qkv_bias, out_bias, up_bias)))
        totals, upstream = lax.scan(run_back, zero_init, (layer_inputs[layer_idx], seg_ids, upstream))
        layer_grads[layer_idx] = totals
    stacked_grads = [jnp.stack([layer_grads[layer_idx][slot_idx] for layer_idx in range(LAYERS)]) for slot_idx in range(9)]
    qkv_new, qkv_states = adamw(w_qkv, stacked_grads[0], qkv_moments, weight_decay)
    dense_new, dense_states = adamw(w_dense, stacked_grads[1], dense_moments, weight_decay)
    up_new, up_states = adamw(w_up, stacked_grads[2], up_moments, weight_decay)
    down_new, down_states = adamw(w_down, stacked_grads[3], down_moments, weight_decay)
    gain_new, gain_states = adamw(norm_gain, stacked_grads[4], gain_moments, 0.0)
    nbias_new, nbias_states = adamw(norm_bias, stacked_grads[5], nbias_moments, 0.0)
    qbias_new, qbias_states = adamw(qkv_bias, stacked_grads[6], qbias_moments, 0.0)
    obias_new, obias_states = adamw(out_bias, stacked_grads[7], obias_moments, 0.0)
    ubias_new, ubias_states = adamw(up_bias, stacked_grads[8], ubias_moments, 0.0)
    return (stream.reshape(TOKENS, D), upstream.reshape(TOKENS, D), stacked_grads[0], stacked_grads[1], stacked_grads[2], stacked_grads[3], stacked_grads[4], stacked_grads[5], stacked_grads[6], stacked_grads[7], stacked_grads[8], qkv_new, dense_new, up_new, down_new, gain_new, nbias_new, qbias_new, obias_new, ubias_new, qkv_states, dense_states, up_states, down_states, gain_states, nbias_states, qbias_states, obias_states, ubias_states)
```

```python
import functools

import jax
import jax.numpy as jnp
from jax import lax
from jax.experimental import pallas as pl
from jax.experimental.pallas import tpu as pltpu
from jax.sharding import PartitionSpec as P

HEADS = 16
HD = 64


norm_eps = 1e-05
beta_first = 0.9
beta_second = 0.999
adam_eps = 1e-08
learn_rate = 0.01
weight_decay = 0.1
adam_step = 3.0
gelu_scale = 0.7978845608028654
gelu_cubic = 0.044715
contract_cols = (((1,), (1,)), ((), ()))
contract_rows = (((0,), (0,)), ((), ()))


def layer_norm(values, gain_vec, shift_vec):
    centered = values - jnp.mean(values, axis=-1, keepdims=True)
    inv_std = lax.rsqrt(jnp.mean(centered * centered, axis=-1, keepdims=True) + norm_eps)
    normed = centered * inv_std
    return (normed * gain_vec + shift_vec, normed, inv_std)


def norm_backward(upstream, normed, inv_std, gain_vec):
    scaled = upstream * gain_vec
    mean_one = jnp.mean(scaled, axis=-1, keepdims=True)
    mean_two = jnp.mean(scaled * normed, axis=-1, keepdims=True)
    return inv_std * (scaled - mean_one - normed * mean_two)


def gelu_parts(pre_act):
    inner_arg = gelu_scale * (pre_act + gelu_cubic * pre_act * pre_act * pre_act)
    tangent = jnp.tanh(inner_arg)
    result = 0.5 * pre_act * (1.0 + tangent)
    deriv = 0.5 * (1.0 + tangent) + 0.5 * pre_act * (1.0 - tangent * tangent) * gelu_scale * (
        1.0 + 3.0 * gelu_cubic * pre_act * pre_act
    )
    return (result, deriv)


def split_heads(joined):
    row_count = joined.shape[0]
    head_count = joined.shape[1] // (3 * HD)
    pieces = joined.reshape(row_count, head_count, 3, HD)
    return (pieces[:, :, 0], pieces[:, :, 1], pieces[:, :, 2])


def masked_scores(queries, key_rows, seg_row, slopes):
    row_count = queries.shape[0]
    scores = jnp.einsum(
        "qhe,khe->hqk", queries, key_rows, preferred_element_type=jnp.float32
    ) * HD ** (-0.5)
    position = jnp.arange(row_count, dtype=jnp.int32)
    offset = (position[None, :] - position[:, None]).astype(jnp.float32)
    scores = scores + slopes[:, None, None] * offset[None]
    allowed = (position[None, :] <= position[:, None]) & (seg_row[:, None] == seg_row[None, :])
    return jnp.where(allowed[None], scores, -jnp.inf)


def attend(joined, seg_row, slopes):
    queries, key_rows, value_rows = split_heads(joined)
    scores = masked_scores(queries, key_rows, seg_row, slopes)
    highest = jnp.max(scores, axis=-1, keepdims=True)
    log_total = highest + jnp.log(jnp.sum(jnp.exp(scores - highest), axis=-1, keepdims=True))
    weights = jnp.exp(scores - log_total).astype(jnp.bfloat16)
    mixed = jnp.einsum("hqk,khe->qhe", weights, value_rows, preferred_element_type=jnp.float32)
    return (mixed.astype(jnp.bfloat16).reshape(joined.shape[0], -1), log_total)


def attend_backward(grad_mix, joined, mixed, log_total, seg_row, slopes):
    queries, key_rows, value_rows = split_heads(joined)
    row_count = joined.shape[0]
    head_count = queries.shape[1]
    scores = masked_scores(queries, key_rows, seg_row, slopes)
    probs = jnp.exp(scores - log_total)
    weights = probs.astype(jnp.bfloat16)
    grad_heads = grad_mix.reshape(row_count, head_count, HD)
    grad_values = jnp.einsum(
        "hqk,qhe->khe", weights, grad_heads, preferred_element_type=jnp.float32
    )
    grad_probs = jnp.einsum(
        "qhe,khe->hqk", grad_heads, value_rows, preferred_element_type=jnp.float32
    )
    delta = jnp.sum(
        grad_heads.astype(jnp.float32)
        * mixed.reshape(row_count, head_count, HD).astype(jnp.float32),
        axis=-1,
    )
    grad_scores = (probs * (grad_probs - jnp.transpose(delta)[:, :, None])).astype(jnp.bfloat16)
    grad_queries = jnp.einsum(
        "hqk,khe->qhe", grad_scores, key_rows, preferred_element_type=jnp.float32
    ) * HD ** (-0.5)
    grad_keys = jnp.einsum(
        "hqk,qhe->khe", grad_scores, queries, preferred_element_type=jnp.float32
    ) * HD ** (-0.5)
    return jnp.stack([grad_queries, grad_keys, grad_values], axis=2).reshape(row_count, -1)


def greet_peers(own, count):
    barrier = pltpu.get_barrier_semaphore()
    for step in range(1, count):
        pl.semaphore_signal(
            barrier,
            inc=1,
            device_id={"mp": lax.rem(own + step, count)},
            device_id_type=pl.DeviceIdType.MESH,
        )
    pl.semaphore_wait(barrier, count - 1)


def gather_kernel(count, rows_ref, out_ref, send_sems, recv_sems):
    own = lax.axis_index("mp")
    rows = rows_ref.shape[0]
    greet_peers(own, count)

    def block_of(index):
        return out_ref.at[pl.ds(pl.multiple_of(index * rows, rows), rows)]

    copies = []
    for step in range(1, count):
        copy = pltpu.make_async_remote_copy(
            src_ref=rows_ref,
            dst_ref=block_of(own),
            send_sem=send_sems.at[step - 1],
            recv_sem=recv_sems.at[step - 1],
            device_id={"mp": lax.rem(own + step, count)},
            device_id_type=pl.DeviceIdType.MESH,
        )
        copy.start()
        copies.append(copy)
    out_ref[pl.ds(pl.multiple_of(own * rows, rows), rows), :] = rows_ref[...]
    for copy in copies:
        copy.wait()


def scatter_kernel(count, parts_ref, out_ref, landed, send_sems, recv_sems):
    own = lax.axis_index("mp")
    rows = out_ref.shape[0]
    greet_peers(own, count)
    copies = []
    for step in range(1, count):
        dest = lax.rem(own + step, count)
        copy = pltpu.make_async_remote_copy(
            src_ref=parts_ref.at[pl.ds(pl.multiple_of(dest * rows, rows), rows)],
            dst_ref=landed.at[step - 1],
            send_sem=send_sems.at[step - 1],
            recv_sem=recv_sems.at[step - 1],
            device_id={"mp": dest},
            device_id_type=pl.DeviceIdType.MESH,
        )
        copy.start()
        copies.append(copy)
    for copy in copies:
        copy.wait()
    total = parts_ref[pl.ds(pl.multiple_of(own * rows, rows), rows), :].astype(jnp.float32)
    for step in range(1, count):
        total = total + landed[step - 1].astype(jnp.float32)
    out_ref[...] = total


transfer_cost = pl.CostEstimate(flops=0, bytes_accessed=40_000_000, transcendentals=0)


def gather_rows(own_rows):
    count = lax.axis_size("mp")
    rows, cols = own_rows.shape
    return pl.pallas_call(
        functools.partial(gather_kernel, count),
        out_shape=jax.ShapeDtypeStruct((rows * count, cols), own_rows.dtype),
        in_specs=[pl.BlockSpec(memory_space=pltpu.VMEM)],
        out_specs=pl.BlockSpec(memory_space=pltpu.VMEM),
        scratch_shapes=[
            pltpu.SemaphoreType.DMA((count - 1,)),
            pltpu.SemaphoreType.DMA((count - 1,)),
        ],
        compiler_params=pltpu.CompilerParams(collective_id=1, has_side_effects=True),
        cost_estimate=transfer_cost,
        name="gather_rows",
    )(own_rows)


def scatter_rows(parts):
    count = lax.axis_size("mp")
    rows, cols = parts.shape[0] // count, parts.shape[1]
    return pl.pallas_call(
        functools.partial(scatter_kernel, count),
        out_shape=jax.ShapeDtypeStruct((rows, cols), jnp.float32),
        in_specs=[pl.BlockSpec(memory_space=pltpu.VMEM)],
        out_specs=pl.BlockSpec(memory_space=pltpu.VMEM),
        scratch_shapes=[
            pltpu.VMEM((count - 1, rows, cols), parts.dtype),
            pltpu.SemaphoreType.DMA((count - 1,)),
            pltpu.SemaphoreType.DMA((count - 1,)),
        ],
        compiler_params=pltpu.CompilerParams(collective_id=2, has_side_effects=True),
        cost_estimate=transfer_cost,
        name="scatter_rows",
    )(parts)


def gather_norm(normed_rows):
    return gather_rows(normed_rows)


def gather_cot(grad_rows):
    return gather_rows(grad_rows)


def project_sum(left, right):
    parts = lax.dot_general(left, right, contract_cols, preferred_element_type=jnp.float32)
    return scatter_rows(parts.astype(jnp.bfloat16))


def project_back(left, right):
    parts = lax.dot_general(left, right, contract_cols, preferred_element_type=jnp.float32)
    return scatter_rows(parts.astype(jnp.bfloat16))


def local_parts(weight_pairs):
    return tuple(
        (
            lax.dot_general(left_op, right_op, contract_rows, preferred_element_type=jnp.float32)
            for left_op, right_op in weight_pairs
        )
    )


def forward_layer(stream_in, seg_row, matrices, vectors, slopes):
    w_joined, w_proj, w_expand, w_shrink = matrices
    gain_vec, shift_vec, joined_bias, out_shift, expand_bias = vectors
    normed_out, normed_one, inv_one = layer_norm(stream_in, gain_vec[0], shift_vec[0])
    rows_one = gather_norm(normed_out.astype(jnp.bfloat16))
    joined = (jnp.dot(rows_one, w_joined, preferred_element_type=jnp.float32) + joined_bias).astype(
        jnp.bfloat16
    )
    mixed, log_total = attend(joined, seg_row, slopes)
    middle = stream_in + project_sum(mixed, w_proj) + out_shift[0]
    normed_mid, normed_two, inv_two = layer_norm(middle, gain_vec[1], shift_vec[1])
    rows_two = gather_norm(normed_mid.astype(jnp.bfloat16))
    pre_act = jnp.dot(rows_two, w_expand, preferred_element_type=jnp.float32) + expand_bias
    activated, deriv = gelu_parts(pre_act)
    hidden_act = activated.astype(jnp.bfloat16)
    result = middle + project_sum(hidden_act, w_shrink) + out_shift[1]
    return (
        result,
        (
            normed_one,
            inv_one,
            rows_one,
            joined,
            mixed,
            log_total,
            normed_two,
            inv_two,
            rows_two,
            deriv,
            hidden_act,
        ),
    )


def backward_layer(upstream, seg_row, matrices, vectors, saved, slopes, early=None):
    w_joined, w_proj, w_expand, w_shrink = matrices
    gain_vec, shift_vec, joined_bias, out_shift, expand_bias = vectors
    (
        normed_one,
        inv_one,
        rows_one,
        joined,
        mixed,
        log_total,
        normed_two,
        inv_two,
        rows_two,
        deriv,
        hidden_act,
    ) = saved
    grad_rows = gather_cot(upstream.astype(jnp.bfloat16))
    grad_hidden = jnp.dot(grad_rows, w_shrink, preferred_element_type=jnp.float32)
    grad_pre = grad_hidden * deriv
    pre_rounded = grad_pre.astype(jnp.bfloat16)
    grad_norm_two = project_back(pre_rounded, w_expand)
    gain_two = jnp.sum(grad_norm_two * normed_two, axis=0)
    shift_two = jnp.sum(grad_norm_two, axis=0)
    middle = upstream + norm_backward(grad_norm_two, normed_two, inv_two, gain_vec[1])
    early_sums = None
    if early is not None:
        early_parts = local_parts(((rows_two, pre_rounded), (grad_rows, hidden_act)))
        middle, early_sums = early(middle, early_parts)
    grad_rows_one = gather_cot(middle.astype(jnp.bfloat16))
    grad_mixed = jnp.dot(grad_rows_one, w_proj, preferred_element_type=jnp.float32).astype(
        jnp.bfloat16
    )
    grad_joined = attend_backward(grad_mixed, joined, mixed, log_total, seg_row, slopes)
    joined_rounded = grad_joined.astype(jnp.bfloat16)
    grad_norm_one = project_back(joined_rounded, w_joined)
    gain_one = jnp.sum(grad_norm_one * normed_one, axis=0)
    shift_one = jnp.sum(grad_norm_one, axis=0)
    grad_below = middle + norm_backward(grad_norm_one, normed_one, inv_one, gain_vec[0])
    weight_pairs = (
        (rows_one, joined_rounded),
        (grad_rows_one, mixed),
    )
    if early is None:
        weight_pairs = weight_pairs + (
            (rows_two, pre_rounded),
            (grad_rows, hidden_act),
        )
    small_grads = (
        jnp.stack([gain_one, gain_two]),
        jnp.stack([shift_one, shift_two]),
        jnp.sum(grad_joined, axis=0),
        jnp.stack([jnp.sum(middle, axis=0), jnp.sum(upstream, axis=0)]),
        jnp.sum(grad_pre, axis=0),
    )
    return (grad_below, weight_pairs, small_grads, early_sums)


def adamw(weight, gradient, moments, decay):
    first = beta_first * moments[0] + (1.0 - beta_first) * gradient
    second = beta_second * moments[1] + (1.0 - beta_second) * gradient * gradient
    first_hat = first / (1.0 - beta_first**adam_step)
    second_hat = second / (1.0 - beta_second**adam_step)
    updated = weight - learn_rate * (first_hat / (jnp.sqrt(second_hat) + adam_eps) + decay * weight)
    return (updated, jnp.stack([first, second]))


def per_device(
    hidden_in,
    seg_ids,
    cotangent,
    w_qkv,
    w_dense,
    w_up,
    w_down,
    norm_gain,
    norm_bias,
    qkv_bias,
    out_bias,
    up_bias,
    qkv_moments,
    dense_moments,
    up_moments,
    down_moments,
    gain_moments,
    nbias_moments,
    qbias_moments,
    obias_moments,
    ubias_moments,
):
    mp_index = lax.axis_index("mp")
    mp_count = lax.axis_size("mp")
    head_local = HEADS // mp_count
    qkv_cols = w_qkv.shape[2]
    up_cols = w_up.shape[2]
    layer_count = w_qkv.shape[0]
    all_slopes = 2.0 ** (-8.0 * jnp.arange(1, HEADS + 1, dtype=jnp.float32) / HEADS)
    slopes = lax.dynamic_slice_in_dim(all_slopes, mp_index * head_local, head_local)
    seg_row = seg_ids[0]
    qkv_local = lax.dynamic_slice_in_dim(qkv_bias, mp_index * qkv_cols, qkv_cols, axis=1)
    up_local = lax.dynamic_slice_in_dim(up_bias, mp_index * up_cols, up_cols, axis=1)

    def vectors_of(layer_idx):
        return (
            norm_gain[layer_idx],
            norm_bias[layer_idx],
            qkv_local[layer_idx],
            out_bias[layer_idx],
            up_local[layer_idx],
        )

    layer_ids = range(layer_count)
    shards = [
        tuple(w[layer_idx].astype(jnp.bfloat16) for w in (w_qkv, w_dense, w_up, w_down))
        for layer_idx in layer_ids
    ]

    def gather_joined(pieces):
        whole = lax.all_gather(jnp.concatenate(pieces, axis=1), "dp", axis=0, tiled=True)
        return split_cols(whole, [piece.shape[1] for piece in pieces])

    def split_cols(whole, widths):
        taken, start = [], 0
        for width in widths:
            taken.append(lax.slice_in_dim(whole, start, start + width, axis=1))
            start += width
        return tuple(taken)

    matrices_of = []
    for layer_idx in layer_ids:
        if layer_idx == 0:
            matrices_of.append(
                gather_joined(shards[0][:2]) + gather_joined(shards[0][2:])
            )
        else:
            matrices_of.append(gather_joined(shards[layer_idx]))
    stream = hidden_in
    kept_acts = []
    for layer_idx in layer_ids:
        stream, saved = forward_layer(
            stream, seg_row, matrices_of[layer_idx], vectors_of(layer_idx), slopes
        )
        kept_acts.append(saved)
    upstream = cotangent
    reduced = [None] * layer_count
    small_parts = [None] * layer_count
    dp_count = lax.axis_size("dp")
    own_rows = w_qkv.shape[1]
    lanes = 128

    def join_parts(pieces):
        return jnp.concatenate([piece.astype(jnp.bfloat16) for piece in pieces], axis=1)

    def scatter_joined(joined):
        return lax.psum_scatter(joined, "dp", scatter_dimension=0, tiled=True)

    def start_early(middle, early_parts):
        middle, joined = lax.optimization_barrier((middle, join_parts(early_parts)))
        if layer_count > 1:
            joined, reduced[1] = lax.optimization_barrier((joined, reduced[1]))
        return (middle, scatter_joined(joined))

    widths = [qkv_cols, w_dense.shape[2], up_cols, w_down.shape[2]]
    for layer_idx in reversed(layer_ids):
        upstream, weight_pairs, small_grads, early_sum = backward_layer(
            upstream,
            seg_row,
            matrices_of[layer_idx],
            vectors_of(layer_idx),
            kept_acts[layer_idx],
            slopes,
            start_early if layer_idx == 0 else None,
        )
        small_parts[layer_idx] = small_grads
        parts = local_parts(weight_pairs)
        if layer_idx > 0:
            upstream, joined = lax.optimization_barrier((upstream, join_parts(parts)))
            reduced[layer_idx] = scatter_joined(joined)
            continue
        shared_part = jnp.concatenate(
            [jnp.stack([part[i] for part in small_parts]).reshape(-1) for i in (0, 1, 3)]
        )
        local_part = jnp.concatenate(
            [jnp.stack([part[i] for part in small_parts]).reshape(-1) for i in (2, 4)]
        )
        small_vec = jnp.concatenate([shared_part, local_part])
        small_len = small_vec.shape[0]
        small_rows = -(-small_len // (dp_count * lanes))
        small_vec = jnp.pad(small_vec, (0, small_rows * dp_count * lanes - small_len))
        small_block = jnp.pad(
            small_vec.reshape(dp_count, small_rows, lanes),
            ((0, 0), (0, own_rows - small_rows), (0, 0)),
        ).reshape(dp_count * own_rows, lanes)
        joined, early_sum = lax.optimization_barrier(
            (join_parts(parts + (small_block,)), early_sum)
        )
        last_sum = scatter_joined(joined)
        qkv_sum, dense_sum, small_sum = split_cols(
            last_sum.astype(jnp.float32), widths[:2] + [lanes]
        )
        up_sum, down_sum = split_cols(early_sum.astype(jnp.float32), widths[2:])
    reduced = [(qkv_sum, dense_sum, up_sum, down_sum)] + [
        split_cols(summed.astype(jnp.float32), widths) for summed in reduced[1:]
    ]
    qkv_grad = jnp.stack([reduced[layer_idx][0] for layer_idx in layer_ids])
    dense_grad = jnp.stack([reduced[layer_idx][1] for layer_idx in layer_ids])
    up_grad = jnp.stack([reduced[layer_idx][2] for layer_idx in layer_ids])
    down_grad = jnp.stack([reduced[layer_idx][3] for layer_idx in layer_ids])
    small_all = lax.all_gather(small_sum[:small_rows], ("dp", "mp"), axis=0, tiled=True)
    small_all = jnp.transpose(
        small_all.reshape(dp_count, mp_count, small_rows * lanes), (1, 0, 2)
    ).reshape(mp_count, -1)
    shared_len = shared_part.shape[0]
    shared_sum = jnp.sum(small_all[:, :shared_len], axis=0).reshape((3,) + norm_gain.shape)
    gain_grad, nbias_grad, obias_grad = shared_sum[0], shared_sum[1], shared_sum[2]
    qbias_len = layer_count * qkv_cols
    qbias_all = small_all[:, shared_len : shared_len + qbias_len]
    ubias_all = small_all[:, shared_len + qbias_len : small_len]

    def unfold(per_rank, width):
        return jnp.transpose(
            per_rank.reshape(mp_count, layer_count, width), (1, 0, 2)
        ).reshape(layer_count, mp_count * width)

    qbias_grad = unfold(qbias_all, qkv_cols)
    ubias_grad = unfold(ubias_all, up_cols)
    qkv_new, qkv_states = adamw(w_qkv, qkv_grad, qkv_moments, weight_decay)
    dense_new, dense_states = adamw(w_dense, dense_grad, dense_moments, weight_decay)
    up_new, up_states = adamw(w_up, up_grad, up_moments, weight_decay)
    down_new, down_states = adamw(w_down, down_grad, down_moments, weight_decay)
    gain_new, gain_states = adamw(norm_gain, gain_grad, gain_moments, 0.0)
    nbias_new, nbias_states = adamw(norm_bias, nbias_grad, nbias_moments, 0.0)
    qbias_new, qbias_states = adamw(qkv_bias, qbias_grad, qbias_moments, 0.0)
    obias_new, obias_states = adamw(out_bias, obias_grad, obias_moments, 0.0)
    ubias_new, ubias_states = adamw(up_bias, ubias_grad, ubias_moments, 0.0)
    return (
        stream,
        upstream,
        qkv_grad,
        dense_grad,
        up_grad,
        down_grad,
        gain_grad,
        nbias_grad,
        qbias_grad,
        obias_grad,
        ubias_grad,
        qkv_new,
        dense_new,
        up_new,
        down_new,
        gain_new,
        nbias_new,
        qbias_new,
        obias_new,
        ubias_new,
        qkv_states,
        dense_states,
        up_states,
        down_states,
        gain_states,
        nbias_states,
        qbias_states,
        obias_states,
        ubias_states,
    )


def solution(mesh):
    return jax.shard_map(
        per_device,
        mesh=mesh,
        in_specs=(
            P(("dp", "mp"), None),
            P("dp", None),
            P(("dp", "mp"), None),
            P(None, "dp", "mp"),
            P(None, "dp", "mp"),
            P(None, "dp", "mp"),
            P(None, "dp", "mp"),
            P(),
            P(),
            P(),
            P(),
            P(),
            P(None, None, "dp", "mp"),
            P(None, None, "dp", "mp"),
            P(None, None, "dp", "mp"),
            P(None, None, "dp", "mp"),
            P(),
            P(),
            P(),
            P(),
            P(),
        ),
        out_specs=(
            P(("dp", "mp"), None),
            P(("dp", "mp"), None),
            P(None, "dp", "mp"),
            P(None, "dp", "mp"),
            P(None, "dp", "mp"),
            P(None, "dp", "mp"),
            P(),
            P(),
            P(),
            P(),
            P(),
            P(None, "dp", "mp"),
            P(None, "dp", "mp"),
            P(None, "dp", "mp"),
            P(None, "dp", "mp"),
            P(),
            P(),
            P(),
            P(),
            P(),
            P(None, None, "dp", "mp"),
            P(None, None, "dp", "mp"),
            P(None, None, "dp", "mp"),
            P(None, None, "dp", "mp"),
            P(),
            P(),
            P(),
            P(),
            P(),
        ),
        check_vma=False,
    )
```
